128 devices in a mesh: board: 8 (over y, z_lo), crate: 16 (over x, z_hi, core).
Axes of the slice: x: 4, y: 4, z: 4 (z_hi: 2, z_lo: 2; z = z_hi * 2 + z_lo), core: 2. Of those that a mesh axis runs over, the one named last changes fastest.
Arguments:
- voltages: bfloat16 [1024, 530432], P(('board', 'crate')), may hold values from -6 to 6
- gains: float32 [2, 1024, 256], P(None, ('board', 'crate')), may hold values from -4 to 4
- channels: int32 [256], replicated, may hold values from 0 to 1023, as said below
Outputs:
- visibilities: float32 [2, 256, 1024, 1024], P(None, ('board', 'crate'))
The draws below stay inside these ranges and needn't reach their ends.
Inputs may be any that keep to these rules, and one draw needn't show every extreme that they name: `channels`: distinct transform bins below half of 2048, in no particular order; bin 0 and the highest such bin are always among them.
All inputs are finite; a program needn't handle non-finite values.
Results may differ from the reference program's by a relative error of at most 0.0056.
Values may be sent and summed in bfloat16 or wider, within the bound.
No kernel may reach another device: no remote copies, remote signals or barrier semaphores. Data moves between devices by JAX's collectives and lax.ppermute only.
A program may use at most 128 MiB of HBM per device.

```python
import math
import jax
import jax.numpy as jnp
from jax import lax

INPUTS = 1024
NFFT = 2048
CHANNELS = 256
TAPS = 4
FRAMES = 256
SAMPLES = 530432


def draw_channels(key, part):
    half = NFFT // 2
    middle = (jax.random.permutation(jax.random.fold_in(key, 11), half - 2)[:CHANNELS - 2] + 1).astype(jnp.int32)
    ends = jnp.array([0, half - 1], jnp.int32)
    full = jnp.concatenate([middle, ends])
    order = jax.random.permutation(jax.random.fold_in(key, 12), CHANNELS)
    return full[order].astype(jnp.int32)


def block_levels(stream_key, shape, pieces, smallest, high):
    def one(dim, blocks):
        steps = jax.random.uniform(jax.random.fold_in(jax.random.fold_in(stream_key, 6), dim), (blocks,), jnp.float32, smallest / len(pieces), high / len(pieces))
        return jnp.repeat(jnp.exp(steps), shape[dim] // blocks).reshape((-1,) + (1,) * (len(shape) - dim - 1))

    loudness = one(*pieces[0])
    for cut in pieces[1:]:
        loudness = loudness * one(*cut)
    return loudness


def bell_draw(key, dims, width, reach, split=(), kind=jnp.bfloat16):
    drawn = width * jax.random.normal(key, dims, jnp.float32)
    if split:
        drawn = drawn * block_levels(key, dims, split, -0.22, 0.18)
    return jnp.clip(drawn, -reach, reach).astype(kind)


def setup_inputs(seed: int = 0) -> dict:
    arg_keys = jax.random.split(jax.random.key(seed), 4)
    return {
        "voltages": bell_draw(arg_keys[0], (INPUTS, SAMPLES), 1.0, 6.0, ((0, 128),)),
        "gains": bell_draw(arg_keys[1], (2, INPUTS, CHANNELS), 1.0, 4.0, ((1, 128),), jnp.float32),
        "channels": draw_channels(jax.random.fold_in(arg_keys[3], 71), 0),
    }


def make_window():
    index = jnp.arange(TAPS * NFFT).astype(jnp.float32)
    centred = (index - TAPS * NFFT / 2 + 0.5) / NFFT
    hamming = 0.54 - 0.46 * jnp.cos(2.0 * jnp.pi * index / (TAPS * NFFT - 1))
    return (jnp.sinc(centred) * hamming).reshape(TAPS, NFFT)

def make_table(channels):
    sample = jnp.arange(NFFT, dtype=jnp.int32)
    phase = sample[:, None] * channels.astype(jnp.int32)[None, :] % NFFT
    angle = phase.astype(jnp.float32) * (2.0 * jnp.pi / NFFT)
    scale = 1.0 / math.sqrt(NFFT)
    return jnp.concatenate([jnp.cos(angle) * scale, -jnp.sin(angle) * scale], axis=1).astype(jnp.bfloat16)

def front_end(group_volts, group_gains, dft_table, window):
    count = group_volts.shape[0]
    framed = group_volts.reshape(count, FRAMES + TAPS - 1, NFFT)
    filtered = jnp.zeros((count, FRAMES, NFFT), jnp.float32)
    for offset in range(TAPS):
        filtered = filtered + window[offset][None, None, :] * framed[:, offset:offset + FRAMES, :].astype(jnp.float32)
    filtered = filtered.astype(jnp.bfloat16)
    raw = jnp.einsum('nk,ifn->kif', dft_table.astype(jnp.float32), filtered.astype(jnp.float32))
    raw = raw.reshape(2, CHANNELS, count, FRAMES)
    gain_real = group_gains[0].T[:, :, None]
    gain_imag = group_gains[1].T[:, :, None]
    out_real = gain_real * raw[0] - gain_imag * raw[1]
    out_imag = gain_real * raw[1] + gain_imag * raw[0]
    return jnp.stack([out_real, out_imag], axis=1).astype(jnp.bfloat16)

def correlate(spectrum):
    part_real = spectrum[0]
    part_imag = spectrum[1]
    stacked = jnp.concatenate([part_real, part_imag], axis=1)
    rotated = jnp.concatenate([part_imag, -part_real], axis=1)
    vis_real = jnp.dot(stacked, stacked.T, preferred_element_type=jnp.float32) / FRAMES
    vis_imag = jnp.dot(rotated, stacked.T, preferred_element_type=jnp.float32) / FRAMES
    return jnp.stack([vis_real, vis_imag], axis=0)

def reference(voltages, gains, channels):
    window = make_window()
    dft_table = make_table(channels)
    groups = INPUTS // 8
    grouped_volts = voltages.reshape(groups, 8, SAMPLES)
    grouped_gains = jnp.transpose(gains.reshape(2, groups, 8, CHANNELS), (1, 0, 2, 3))
    spectra = lax.map(lambda pair: front_end(pair[0], pair[1], dft_table, window), (grouped_volts, grouped_gains))
    spectra = jnp.transpose(spectra, (1, 2, 0, 3, 4)).reshape(CHANNELS, 2, INPUTS, FRAMES)
    result = lax.map(correlate, spectra)
    return jnp.transpose(result, (1, 0, 2, 3))
```

```python
import math

import jax
import jax.numpy as jnp
from jax import lax
from jax.experimental import pallas as pl
from jax.experimental.pallas import tpu as pltpu
from jax.sharding import PartitionSpec as P

NFFT = 2048
TAPS = 4
LANES = 128
CHUNK = 32
COARSE = 64


def make_window(taps_count, length):
    index = jnp.arange(taps_count * length).astype(jnp.float32)
    centred = (index - taps_count * length / 2 + 0.5) / length
    hamming = 0.54 - 0.46 * jnp.cos(2.0 * jnp.pi * index / (taps_count * length - 1))
    return (jnp.sinc(centred) * hamming).reshape(taps_count, length)


def phasor(rows, channels):
    phase = (rows * channels) & (NFFT - 1)
    quarter = NFFT // 4
    turn = (phase + quarter // 2) // quarter
    angle = (phase - turn * quarter).astype(jnp.float32) * (2.0 * math.pi / NFFT)
    square = angle * angle
    sine = angle * (
        1.0 + square * (-1 / 6 + square * (1 / 120 + square * (-1 / 5040 + square * (1 / 362880))))
    )
    cosine = 1.0 + square * (
        -1 / 2
        + square * (1 / 24 + square * (-1 / 720 + square * (1 / 40320 - square * (1 / 3628800))))
    )
    swap = (turn & 1) == 1
    turned_cos = jnp.where(swap, sine, cosine)
    turned_sin = jnp.where(swap, cosine, sine)
    cos_sign = jnp.where(((turn + 1) & 2) == 2, -1.0, 1.0)
    sin_sign = jnp.where((turn & 2) == 2, -1.0, 1.0)
    return turned_cos * cos_sign, turned_sin * sin_sign


def front_kernel(v_hbm, window, channels, gains, out, volts, table, filtered, raw, turned, sems):
    inputs = out.shape[2]
    kept = out.shape[0]
    frames = out.shape[3]
    chunks = frames // CHUNK
    span = CHUNK * NFFT
    rows = CHUNK * inputs
    tail = (TAPS - 1) * NFFT

    def piece(k):
        start = 0 if k == 0 else tail + k * span
        size = span + tail if k == 0 else span
        return pltpu.make_async_copy(
            v_hbm.at[:, pl.ds(start, size)], volts.at[:, pl.ds(start, size)], sems.at[k]
        )

    for k in range(chunks):
        piece(k).start()

    scale = 1.0 / math.sqrt(NFFT)
    for half in range(kept // LANES):
        lanes = pl.ds(half * LANES, LANES)
        bins = channels[:, lanes]
        fine_cos, fine_sin = phasor(lax.broadcasted_iota(jnp.int32, (COARSE, LANES), 0), bins)
        fine_cos, fine_sin = fine_cos * scale, fine_sin * scale
        steps = NFFT // COARSE
        coarse_cos_all, coarse_sin_all = phasor(
            lax.broadcasted_iota(jnp.int32, (steps, LANES), 0) * COARSE, bins
        )

        for a in range(steps):
            coarse_cos = coarse_cos_all[a : a + 1]
            coarse_sin = coarse_sin_all[a : a + 1]
            at = pl.ds(a * COARSE, COARSE)
            table[at, lanes] = (fine_cos * coarse_cos - fine_sin * coarse_sin).astype(
                jnp.bfloat16
            )
            table[at, pl.ds(kept + half * LANES, LANES)] = (
                -(fine_sin * coarse_cos + fine_cos * coarse_sin)
            ).astype(jnp.bfloat16)

    for k in range(chunks):
        piece(k).wait()

        @pl.loop(0, NFFT // LANES)
        def _(j):
            lane = pl.multiple_of(j * LANES, LANES)
            taps = [
                jnp.broadcast_to(window[t : t + 1, pl.ds(lane, LANES)], (inputs, LANES))
                for t in range(TAPS)
            ]

            def load(f):
                at = pl.multiple_of(lane + (k * CHUNK + f) * NFFT, LANES)
                return volts[:, pl.ds(at, LANES)].astype(jnp.float32)

            held = [load(f) for f in range(TAPS - 1)]
            for f in range(0, CHUNK, 2):
                pair = []
                for g in (f, f + 1):
                    held.append(load(g + TAPS - 1))
                    total = taps[0] * held[0]
                    for t in range(1, TAPS):
                        total = total + taps[t] * held[t]
                    held.pop(0)
                    pair.append(total)
                filtered[pl.ds(f * inputs, 2 * inputs), pl.ds(lane, LANES)] = jnp.concatenate(
                    pair, axis=0
                ).astype(jnp.bfloat16)

        product = jnp.dot(filtered[...], table[...], preferred_element_type=jnp.float32)
        for q in range(2 * kept // LANES):
            raw[q, pl.ds(k * rows, rows), :] = product[:, q * LANES : (q + 1) * LANES]

    for half in range(kept // LANES):
        lanes = pl.ds(half * LANES, LANES)
        for block in range(frames // LANES):
            for i in range(inputs):
                at = pl.ds(block * LANES * inputs + i, LANES, stride=inputs)
                gain_real = gains[0, i : i + 1, lanes]
                gain_imag = gains[1, i : i + 1, lanes]
                real = raw[half, at, :]
                imag = raw[half + kept // LANES, at, :]
                turned[0, pl.ds(i, LANES, stride=inputs), :] = (
                    gain_real * real - gain_imag * imag
                ).T
                turned[1, pl.ds(i, LANES, stride=inputs), :] = (
                    gain_real * imag + gain_imag * real
                ).T
            for part in range(2):
                out[
                    pl.ds(half * LANES, LANES), part, :, pl.ds(block * LANES, LANES)
                ] = turned[part].reshape(LANES, inputs, LANES).astype(jnp.bfloat16)


def front_end(voltages, gains, channels):
    inputs, samples = voltages.shape
    frames = samples // NFFT - TAPS + 1
    kept = channels.shape[0]
    window = make_window(TAPS, NFFT)
    vmem = pl.BlockSpec(memory_space=pltpu.VMEM)
    return pl.pallas_call(
        front_kernel,
        out_shape=jax.ShapeDtypeStruct((kept, 2, inputs, frames), jnp.bfloat16),
        in_specs=[pl.BlockSpec(memory_space=pltpu.HBM), vmem, vmem, vmem],
        out_specs=vmem,
        scratch_shapes=[
            pltpu.VMEM((inputs, samples), jnp.bfloat16),
            pltpu.VMEM((NFFT, 2 * kept), jnp.bfloat16),
            pltpu.VMEM((CHUNK * inputs, NFFT), jnp.bfloat16),
            pltpu.VMEM((2 * kept // LANES, frames * inputs, LANES), jnp.float32),
            pltpu.VMEM((2, LANES * inputs, LANES), jnp.float32),
            pltpu.SemaphoreType.DMA((frames // CHUNK,)),
        ],
        compiler_params=pltpu.CompilerParams(vmem_limit_bytes=60 * 2**20),
        cost_estimate=pl.CostEstimate(
            flops=4 * frames * inputs * NFFT * kept,
            bytes_accessed=2 * inputs * samples,
            transcendentals=0,
        ),
        name="front_end",
    )(voltages, window, channels.reshape(1, kept), gains)


def correlate_kernel(spectra, out, rows):
    sources, _, _, inputs, frames = spectra.shape
    total = sources * inputs
    width = out.shape[3]
    step = pl.program_id(1)

    @pl.when(step == 0)
    def _():
        c = pl.program_id(0)
        real = spectra[:, c, 0].reshape(total, frames)
        imag = spectra[:, c, 1].reshape(total, frames)
        rows[pl.ds(0, total), pl.ds(0, frames)] = real
        rows[pl.ds(0, total), pl.ds(frames, frames)] = imag
        rows[pl.ds(total, total), pl.ds(0, frames)] = imag
        rows[pl.ds(total, total), pl.ds(frames, frames)] = -real

    at = pl.ds(pl.multiple_of(step * width, width), width)
    product = lax.dot_general(
        rows[...],
        rows[at, :],
        (((1,), (1,)), ((), ())),
        preferred_element_type=jnp.float32,
    )
    out[0, 0] = product[:total] / frames
    out[1, 0] = product[total:] / frames


def correlate(spectra):
    sources, owned, _, inputs, frames = spectra.shape
    total = sources * inputs
    width = 256
    return pl.pallas_call(
        correlate_kernel,
        grid=(owned, total // width),
        out_shape=jax.ShapeDtypeStruct((2, owned, total, total), jnp.float32),
        in_specs=[pl.BlockSpec(memory_space=pltpu.VMEM)],
        out_specs=pl.BlockSpec((2, 1, total, width), lambda c, r: (0, c, 0, r)),
        scratch_shapes=[pltpu.VMEM((2 * total, 2 * frames), jnp.bfloat16)],
        compiler_params=pltpu.CompilerParams(
            dimension_semantics=("arbitrary", "arbitrary"), vmem_limit_bytes=40 * 2**20
        ),
        cost_estimate=pl.CostEstimate(
            flops=8 * owned * total * total * frames,
            bytes_accessed=8 * owned * total * total,
            transcendentals=0,
        ),
        name="correlate",
    )(spectra)


def solution(mesh):
    devices = mesh.size
    axes = ("board", "crate")

    def local(voltages, gains, channels):
        spectra = front_end(voltages, gains, channels)
        kept = spectra.shape[0]
        split = spectra.reshape(devices, kept // devices, *spectra.shape[1:])
        return correlate(lax.all_to_all(split, axes, 0, 0, tiled=True))

    placed = (P(axes, None), P(None, axes, None), P())
    return jax.shard_map(
        local,
        mesh=mesh,
        in_specs=placed,
        out_specs=P(None, axes, None, None),
        check_vma=False,
    )
```

```python
import math

import jax
import jax.numpy as jnp
import numpy as np
from jax import lax
from jax.experimental import pallas as pl
from jax.experimental.pallas import tpu as pltpu
from jax.sharding import PartitionSpec as P

NFFT = 2048
TAPS = 4
LANES = 128
WIDE = 256
CHUNK = 32
COARSE = 64


def make_window(taps_count, length):
    index = np.arange(taps_count * length, dtype=np.float64)
    centred = (index - taps_count * length / 2 + 0.5) / length
    hamming = 0.54 - 0.46 * np.cos(2.0 * np.pi * index / (taps_count * length - 1))
    return (np.sinc(centred) * hamming).reshape(taps_count, length).astype(np.float32)


def phasor(rows, channels):
    phase = (rows * channels) & (NFFT - 1)
    quarter = NFFT // 4
    turn = (phase + quarter // 2) // quarter
    angle = (phase - turn * quarter).astype(jnp.float32) * (2.0 * math.pi / NFFT)
    square = angle * angle
    sine = angle * (
        1.0 + square * (-1 / 6 + square * (1 / 120 + square * (-1 / 5040 + square * (1 / 362880))))
    )
    cosine = 1.0 + square * (
        -1 / 2
        + square * (1 / 24 + square * (-1 / 720 + square * (1 / 40320 - square * (1 / 3628800))))
    )
    swap = (turn & 1) == 1
    turned_cos = jnp.where(swap, sine, cosine)
    turned_sin = jnp.where(swap, cosine, sine)
    cos_sign = jnp.where(((turn + 1) & 2) == 2, -1.0, 1.0)
    sin_sign = jnp.where((turn & 2) == 2, -1.0, 1.0)
    return turned_cos * cos_sign, turned_sin * sin_sign


def front_kernel(
    v_hbm, window_hbm, channels_hbm, gains_hbm, out,
    volts, window, channels, gains, table, even, odd, raw, turned, sems, small_sems,
):
    inputs = out.shape[2]
    kept = out.shape[0]
    frames = out.shape[3]
    chunks = frames // CHUNK
    span = CHUNK * NFFT
    rows = CHUNK * inputs
    tail = (TAPS - 1) * NFFT
    parts = kept // LANES

    def piece(k):
        at = pl.ds(tail + k * span, span)
        return pltpu.make_async_copy(v_hbm.at[:, at], volts.at[:, at], sems.at[k])

    head = pltpu.make_async_copy(
        v_hbm.at[:, pl.ds(0, tail)], volts.at[:, pl.ds(0, tail)], sems.at[chunks]
    )
    small = [
        pltpu.make_async_copy(source, target, small_sems.at[n])
        for n, (source, target) in enumerate(
            ((channels_hbm, channels), (window_hbm, window), (gains_hbm, gains))
        )
    ]
    small[0].start()
    head.start()
    small[1].start()
    for k in range(chunks):
        piece(k).start()
    small[2].start()

    scale = 1.0 / math.sqrt(NFFT)
    steps = NFFT // 2 // COARSE
    small[0].wait()
    for part in range(parts):
        lanes = pl.ds(part * LANES, LANES)
        others = pl.ds(kept + part * LANES, LANES)
        bins = channels[:, lanes]
        fine_cos, fine_sin = phasor(lax.broadcasted_iota(jnp.int32, (COARSE, LANES), 0), bins)
        fine_cos, fine_sin = fine_cos * scale, fine_sin * -scale
        coarse_cos, coarse_sin = phasor(
            lax.broadcasted_iota(jnp.int32, (steps, LANES), 0) * COARSE, bins
        )
        sign = jnp.where((bins & 1) == 1, -1.0, 1.0).astype(jnp.bfloat16)
        for a in range(steps):
            cos_a = coarse_cos[a : a + 1]
            sin_a = coarse_sin[a : a + 1]
            real = (fine_cos * cos_a + fine_sin * sin_a).astype(jnp.bfloat16)
            imag = (fine_sin * cos_a - fine_cos * sin_a).astype(jnp.bfloat16)
            table[pl.ds(a * COARSE, COARSE), lanes] = real
            table[pl.ds(a * COARSE, COARSE), others] = imag
            table[pl.ds(NFFT // 2 + a * COARSE, COARSE), lanes] = real * sign
            table[pl.ds(NFFT // 2 + a * COARSE, COARSE), others] = imag * sign

    def filter_tile(k, target, lane):
        taps = [
            jnp.broadcast_to(window[t : t + 1, pl.ds(lane, WIDE)], (inputs, WIDE))
            for t in range(TAPS)
        ]

        def load(f):
            at = (k * CHUNK + f) * NFFT + lane
            if not isinstance(at, int):
                at = pl.multiple_of(at, LANES)
            return volts[:, pl.ds(at, WIDE)].astype(jnp.float32)

        held = [load(f) for f in range(TAPS - 1)]
        for f in range(0, CHUNK, 2):
            pair = []
            for g in (f, f + 1):
                held.append(load(g + TAPS - 1))
                total = taps[0] * held[0]
                for t in range(1, TAPS):
                    total = total + taps[t] * held[t]
                held.pop(0)
                pair.append(total)
            target[pl.ds(f * inputs, 2 * inputs), pl.ds(lane, WIDE)] = jnp.concatenate(
                pair, axis=0
            ).astype(jnp.bfloat16)

    def transform(k, source):
        product = jnp.dot(source[...], table[...], preferred_element_type=jnp.float32)
        at = pl.ds(k * rows, rows)
        for q in range(2 * parts):
            raw[q, at, :] = product[:, q * LANES : (q + 1) * LANES]

    def both(k, source, target):
        transform(k, source)
        for j in range(NFFT // WIDE):
            filter_tile(k + 1, target, j * WIDE)

    small[1].wait()
    head.wait()
    piece(0).wait()

    @pl.loop(0, NFFT // WIDE)
    def _(j):
        filter_tile(0, even, pl.multiple_of(j * WIDE, WIDE))

    small[2].wait()
    early = chunks // 2
    for k in range(1, early):
        piece(k).wait()
    for k in range(chunks - 1):
        if k + 1 == early:
            for later in range(early, chunks):
                piece(later).wait()
        both(k, *((even, odd) if k % 2 == 0 else (odd, even)))
    transform(chunks - 1, even if chunks % 2 == 1 else odd)

    for part in range(parts):
        lanes = pl.ds(part * LANES, LANES)
        for block in range(frames // LANES):
            for i in range(inputs):
                at = pl.ds(block * LANES * inputs + i, LANES, stride=inputs)
                gain_real = gains[0, i : i + 1, lanes]
                gain_imag = gains[1, i : i + 1, lanes]
                real = raw[part, at, :]
                imag = raw[part + parts, at, :]
                turned[0, pl.ds(i, LANES, stride=inputs), :] = (
                    gain_real * real - gain_imag * imag
                ).T
                turned[1, pl.ds(i, LANES, stride=inputs), :] = (
                    gain_real * imag + gain_imag * real
                ).T
            for side in range(2):
                out[
                    pl.ds(part * LANES, LANES), side, :, pl.ds(block * LANES, LANES)
                ] = turned[side].reshape(LANES, inputs, LANES).astype(jnp.bfloat16)


def front_end(voltages, gains, channels):
    inputs, samples = voltages.shape
    frames = samples // NFFT - TAPS + 1
    kept = channels.shape[0]
    window = jnp.asarray(make_window(TAPS, NFFT))
    hbm = pl.BlockSpec(memory_space=pltpu.HBM)
    return pl.pallas_call(
        front_kernel,
        out_shape=jax.ShapeDtypeStruct((kept, 2, inputs, frames), jnp.bfloat16),
        in_specs=[hbm] * 4,
        out_specs=pl.BlockSpec(memory_space=pltpu.VMEM),
        scratch_shapes=[
            pltpu.VMEM((inputs, samples), jnp.bfloat16),
            pltpu.VMEM((TAPS, NFFT), jnp.float32),
            pltpu.VMEM((1, kept), jnp.int32),
            pltpu.VMEM((2, inputs, kept), jnp.float32),
            pltpu.VMEM((NFFT, 2 * kept), jnp.bfloat16),
            pltpu.VMEM((CHUNK * inputs, NFFT), jnp.bfloat16),
            pltpu.VMEM((CHUNK * inputs, NFFT), jnp.bfloat16),
            pltpu.VMEM((2 * kept // LANES, frames * inputs, LANES), jnp.float32),
            pltpu.VMEM((2, LANES * inputs, LANES), jnp.float32),
            pltpu.SemaphoreType.DMA((frames // CHUNK + 1,)),
            pltpu.SemaphoreType.DMA((3,)),
        ],
        compiler_params=pltpu.CompilerParams(vmem_limit_bytes=50 * 2**20),
        cost_estimate=pl.CostEstimate(
            flops=4 * frames * inputs * NFFT * kept,
            bytes_accessed=2 * inputs * samples,
            transcendentals=0,
        ),
        name="front_end",
    )(
        voltages,
        *(
            pltpu.with_memory_space_constraint(x, pltpu.HBM)
            for x in (window, channels.reshape(1, kept), gains)
        ),
    )


def correlate_kernel(spectra, out, rows, blocks, sems):
    sources, owned, _, inputs, frames = spectra.shape
    total = sources * inputs
    side = blocks.shape[-1]
    across = total // side
    contract = (((1,), (1,)), ((), ()))

    for c in range(owned):
        real = spectra[:, c, 0].reshape(total, frames)
        imag = spectra[:, c, 1].reshape(total, frames)
        rows[c, 0, :, pl.ds(0, frames)] = real
        rows[c, 0, :, pl.ds(frames, frames)] = imag
        rows[c, 1, :, pl.ds(0, frames)] = imag
        rows[c, 1, :, pl.ds(frames, frames)] = -real

    def copies(c, a, b, slot):
        every = []
        for n, (row, column) in enumerate(((a, b), (b, a)) if a != b else ((a, b),)):
            every.append(
                pltpu.make_async_copy(
                    blocks.at[slot, n],
                    out.at[:, c, pl.ds(row * side, side), pl.ds(column * side, side)],
                    sems.at[slot, n],
                )
            )
        return every

    slots = blocks.shape[0]
    flying = []
    for c in range(owned):
        for b in range(across):
            for a in range(b, across):
                step = len(flying)
                slot = step % slots
                if step >= slots:
                    for copy in flying[step - slots]:
                        copy.wait()
                weights = rows[c, 0, pl.ds(b * side, side), :]
                for part in range(2):
                    block = lax.dot_general(
                        rows[c, part, pl.ds(a * side, side), :],
                        weights,
                        contract,
                        preferred_element_type=jnp.float32,
                    ) / frames
                    blocks[slot, 0, part] = block
                    if a != b:
                        mirror = block.T
                        blocks[slot, 1, part] = mirror if part == 0 else -mirror
                started = copies(c, a, b, slot)
                for copy in started:
                    copy.start()
                flying.append(started)
    for started in flying[-slots:]:
        for copy in started:
            copy.wait()


def correlate(spectra):
    sources, owned, _, inputs, frames = spectra.shape
    total = sources * inputs
    side = 256
    slots = 6
    return pl.pallas_call(
        correlate_kernel,
        out_shape=jax.ShapeDtypeStruct((2, owned, total, total), jnp.float32),
        in_specs=[pl.BlockSpec(memory_space=pltpu.VMEM)],
        out_specs=pl.BlockSpec(memory_space=pltpu.HBM),
        scratch_shapes=[
            pltpu.VMEM((owned, 2, total, 2 * frames), jnp.bfloat16),
            pltpu.VMEM((slots, 2, 2, side, side), jnp.float32),
            pltpu.SemaphoreType.DMA((slots, 2)),
        ],
        compiler_params=pltpu.CompilerParams(vmem_limit_bytes=40 * 2**20),
        cost_estimate=pl.CostEstimate(
            flops=8 * owned * total * total * frames,
            bytes_accessed=8 * owned * total * total,
            transcendentals=0,
        ),
        name="correlate",
    )(spectra)


def solution(mesh):
    devices = mesh.size
    axes = ("board", "crate")

    def local(voltages, gains, channels):
        spectra = front_end(voltages, gains, channels)
        kept = spectra.shape[0]
        split = spectra.reshape(devices, kept // devices, *spectra.shape[1:])
        return correlate(lax.all_to_all(split, axes, 0, 0, tiled=True))

    placed = (P(axes, None), P(None, axes, None), P())
    return jax.shard_map(
        local,
        mesh=mesh,
        in_specs=placed,
        out_specs=P(None, axes, None, None),
        check_vma=False,
    )
```

```python
import math

import jax
import jax.numpy as jnp
import numpy as np
from jax import lax
from jax.experimental import pallas as pl
from jax.experimental.pallas import tpu as pltpu
from jax.sharding import PartitionSpec as P

NFFT = 2048
TAPS = 4
LANES = 128
WIDE = 256
CHUNK = 32
COARSE = 64


def make_window(taps_count, length):
    index = np.arange(taps_count * length, dtype=np.float64)
    centred = (index - taps_count * length / 2 + 0.5) / length
    hamming = 0.54 - 0.46 * np.cos(2.0 * np.pi * index / (taps_count * length - 1))
    return (np.sinc(centred) * hamming).reshape(taps_count, length).astype(np.float32)


def phasor(rows, channels):
    phase = (rows * channels) & (NFFT - 1)
    quarter = NFFT // 4
    turn = (phase + quarter // 2) // quarter
    angle = (phase - turn * quarter).astype(jnp.float32) * (2.0 * math.pi / NFFT)
    square = angle * angle
    sine = angle * (
        1.0 + square * (-1 / 6 + square * (1 / 120 + square * (-1 / 5040 + square * (1 / 362880))))
    )
    cosine = 1.0 + square * (
        -1 / 2
        + square * (1 / 24 + square * (-1 / 720 + square * (1 / 40320 - square * (1 / 3628800))))
    )
    swap = (turn & 1) == 1
    turned_cos = jnp.where(swap, sine, cosine)
    turned_sin = jnp.where(swap, cosine, sine)
    cos_sign = jnp.where(((turn + 1) & 2) == 2, -1.0, 1.0)
    sin_sign = jnp.where((turn & 2) == 2, -1.0, 1.0)
    return turned_cos * cos_sign, turned_sin * sin_sign


def front_kernel(
    v_hbm, window_hbm, channels_hbm, gains_hbm, out,
    volts, window, channels, gains, last_gains, table, first, second, third, raw, turned, sems, small_sems,
):
    inputs = out.shape[2]
    kept = out.shape[0]
    frames = out.shape[3]
    chunks = frames // CHUNK
    span = CHUNK * NFFT
    rows = CHUNK * inputs
    tail = (TAPS - 1) * NFFT
    parts = kept // LANES

    def piece(k):
        at = pl.ds(tail + k * span, span)
        return pltpu.make_async_copy(v_hbm.at[:, at], volts.at[:, at], sems.at[k])

    head = pltpu.make_async_copy(
        v_hbm.at[:, pl.ds(0, tail)], volts.at[:, pl.ds(0, tail)], sems.at[chunks]
    )
    small = [
        pltpu.make_async_copy(source, target, small_sems.at[n])
        for n, (source, target) in enumerate(
            (
                (channels_hbm, channels),
                (window_hbm, window),
                (gains_hbm, gains),
                (gains_hbm, last_gains),
            )
        )
    ]
    small[0].start()
    head.start()
    small[1].start()
    for k in range(chunks):
        piece(k).start()
    small[2].start()
    small[3].start()

    scale = 1.0 / math.sqrt(NFFT)
    steps = NFFT // 2 // COARSE
    small[0].wait()
    for part in range(parts):
        lanes = pl.ds(2 * part * LANES, LANES)
        others = pl.ds((2 * part + 1) * LANES, LANES)
        bins = channels[:, pl.ds(part * LANES, LANES)]
        fine_cos, fine_sin = phasor(lax.broadcasted_iota(jnp.int32, (COARSE, LANES), 0), bins)
        fine_cos, fine_sin = fine_cos * scale, fine_sin * -scale
        coarse_cos, coarse_sin = phasor(
            lax.broadcasted_iota(jnp.int32, (steps, LANES), 0) * COARSE, bins
        )
        sign = jnp.where((bins & 1) == 1, -1.0, 1.0).astype(jnp.bfloat16)
        for a in range(steps):
            cos_a = coarse_cos[a : a + 1]
            sin_a = coarse_sin[a : a + 1]
            real = (fine_cos * cos_a + fine_sin * sin_a).astype(jnp.bfloat16)
            imag = (fine_sin * cos_a - fine_cos * sin_a).astype(jnp.bfloat16)
            table[pl.ds(a * COARSE, COARSE), lanes] = real
            table[pl.ds(a * COARSE, COARSE), others] = imag
            table[pl.ds(NFFT // 2 + a * COARSE, COARSE), lanes] = real * sign
            table[pl.ds(NFFT // 2 + a * COARSE, COARSE), others] = imag * sign

    def filter_tile(k, target, lane):
        taps = [
            jnp.broadcast_to(window[t : t + 1, pl.ds(lane, WIDE)], (inputs, WIDE))
            for t in range(TAPS)
        ]

        def load(f):
            at = (k * CHUNK + f) * NFFT + lane
            if not isinstance(at, int):
                at = pl.multiple_of(at, LANES)
            return volts[:, pl.ds(at, WIDE)].astype(jnp.float32)

        held = [load(f) for f in range(TAPS - 1)]
        for f in range(0, CHUNK, 2):
            pair = []
            for g in (f, f + 1):
                held.append(load(g + TAPS - 1))
                total = taps[0] * held[0]
                for t in range(1, TAPS):
                    total = total + taps[t] * held[t]
                held.pop(0)
                pair.append(total)
            target[pl.ds(f * inputs, 2 * inputs), pl.ds(lane, WIDE)] = jnp.concatenate(
                pair, axis=0
            ).astype(jnp.bfloat16)

    def transform(k, pieces):
        source = slots[k % len(slots)]
        width = 2 * kept // pieces
        at = pl.ds(k * rows, rows)
        for n in range(pieces):
            product = jnp.dot(
                source[...],
                table[:, n * width : (n + 1) * width],
                preferred_element_type=jnp.float32,
            )
            for q in range(width // LANES):
                raw[n * width // LANES + q, at, :] = product[:, q * LANES : (q + 1) * LANES]

    slots = (first, second, third)
    ahead = len(slots) - 1
    small[1].wait()
    head.wait()
    for k in range(ahead):
        piece(k).wait()

        @pl.loop(0, NFFT // WIDE)
        def _(j):
            filter_tile(k, slots[k], pl.multiple_of(j * WIDE, WIDE))

    small[2].wait()
    for k in range(ahead, chunks):
        piece(k).wait()
    for k in range(chunks):
        transform(k, parts if k == chunks - 1 else 1)
        if k + ahead < chunks:
            for j in range(NFFT // WIDE):
                filter_tile(k + ahead, slots[(k + ahead) % len(slots)], j * WIDE)

    def turn(part, block, gains):
        lanes = pl.ds(part * LANES, LANES)
        for i in range(inputs):
            at = pl.ds(block * LANES * inputs + i, LANES, stride=inputs)
            gain_real = gains[0, i : i + 1, lanes]
            gain_imag = gains[1, i : i + 1, lanes]
            real = raw[2 * part, at, :]
            imag = raw[2 * part + 1, at, :]
            turned[0, pl.ds(i, LANES, stride=inputs), :] = (
                gain_real * real - gain_imag * imag
            ).T
            turned[1, pl.ds(i, LANES, stride=inputs), :] = (
                gain_real * imag + gain_imag * real
            ).T
        for side in range(2):
            out[pl.ds(part * LANES, LANES), side, :, pl.ds(block * LANES, LANES)] = (
                turned[side].reshape(LANES, inputs, LANES).astype(jnp.bfloat16)
            )

    turns = [(part, block) for block in range(frames // LANES) for part in range(parts)]
    for part, block in turns[:-1]:
        turn(part, block, gains)
    small[3].wait()
    turn(*turns[-1], last_gains)


def front_end(voltages, gains, channels):
    inputs, samples = voltages.shape
    frames = samples // NFFT - TAPS + 1
    kept = channels.shape[0]
    window = jnp.asarray(make_window(TAPS, NFFT))
    hbm = pl.BlockSpec(memory_space=pltpu.HBM)
    return pl.pallas_call(
        front_kernel,
        out_shape=jax.ShapeDtypeStruct((kept, 2, inputs, frames), jnp.bfloat16),
        in_specs=[hbm] * 4,
        out_specs=pl.BlockSpec(memory_space=pltpu.VMEM),
        scratch_shapes=[
            pltpu.VMEM((inputs, samples), jnp.bfloat16),
            pltpu.VMEM((TAPS, NFFT), jnp.float32),
            pltpu.VMEM((1, kept), jnp.int32),
            *[pltpu.VMEM((2, inputs, kept), jnp.float32)] * 2,
            pltpu.VMEM((NFFT, 2 * kept), jnp.bfloat16),
            *[pltpu.VMEM((CHUNK * inputs, NFFT), jnp.bfloat16)] * 3,
            pltpu.VMEM((2 * kept // LANES, frames * inputs, LANES), jnp.float32),
            pltpu.VMEM((2, LANES * inputs, LANES), jnp.float32),
            pltpu.SemaphoreType.DMA((frames // CHUNK + 1,)),
            pltpu.SemaphoreType.DMA((4,)),
        ],
        compiler_params=pltpu.CompilerParams(vmem_limit_bytes=50 * 2**20),
        cost_estimate=pl.CostEstimate(
            flops=4 * frames * inputs * NFFT * kept,
            bytes_accessed=2 * inputs * samples,
            transcendentals=0,
        ),
        name="front_end",
    )(
        voltages,
        *(
            pltpu.with_memory_space_constraint(x, pltpu.HBM)
            for x in (window, channels.reshape(1, kept), gains)
        ),
    )


def correlate_kernel(spectra, out, rows, blocks, sems):
    sources, owned, _, inputs, frames = spectra.shape
    total = sources * inputs
    side = blocks.shape[-1]
    across = total // side
    contract = (((1,), (1,)), ((), ()))

    for c in range(owned):
        real = spectra[:, c, 0].reshape(total, frames)
        imag = spectra[:, c, 1].reshape(total, frames)
        rows[c, 0, :, pl.ds(0, frames)] = real
        rows[c, 0, :, pl.ds(frames, frames)] = imag
        rows[c, 1, :, pl.ds(0, frames)] = imag
        rows[c, 1, :, pl.ds(frames, frames)] = -real

    def copies(c, a, b, slot):
        every = []
        for n, (row, column) in enumerate(((a, b), (b, a)) if a != b else ((a, b),)):
            every.append(
                pltpu.make_async_copy(
                    blocks.at[slot, n],
                    out.at[:, c, pl.ds(row * side, side), pl.ds(column * side, side)],
                    sems.at[slot, n],
                )
            )
        return every

    flying = []
    for c in range(owned):
        for b in range(across):
            for a in range(b, across):
                slot = len(flying)
                weights = rows[c, 0, pl.ds(b * side, side), :]
                for part in range(2):
                    block = lax.dot_general(
                        rows[c, part, pl.ds(a * side, side), :],
                        weights,
                        contract,
                        preferred_element_type=jnp.float32,
                    ) / frames
                    blocks[slot, 0, part] = block
                    if a != b:
                        mirror = block.T
                        blocks[slot, 1, part] = mirror if part == 0 else -mirror
                started = copies(c, a, b, slot)
                for copy in started:
                    copy.start()
                flying.append(started)
    for started in flying:
        for copy in started:
            copy.wait()


def correlate(spectra):
    sources, owned, _, inputs, frames = spectra.shape
    total = sources * inputs
    side = 256
    across = total // side
    slots = owned * across * (across + 1) // 2
    return pl.pallas_call(
        correlate_kernel,
        out_shape=jax.ShapeDtypeStruct((2, owned, total, total), jnp.float32),
        in_specs=[pl.BlockSpec(memory_space=pltpu.VMEM)],
        out_specs=pl.BlockSpec(memory_space=pltpu.HBM),
        scratch_shapes=[
            pltpu.VMEM((owned, 2, total, 2 * frames), jnp.bfloat16),
            pltpu.VMEM((slots, 2, 2, side, side), jnp.float32),
            pltpu.SemaphoreType.DMA((slots, 2)),
        ],
        compiler_params=pltpu.CompilerParams(vmem_limit_bytes=48 * 2**20),
        cost_estimate=pl.CostEstimate(
            flops=8 * owned * total * total * frames,
            bytes_accessed=8 * owned * total * total,
            transcendentals=0,
        ),
        name="correlate",
    )(spectra)


def solution(mesh):
    devices = mesh.size
    axes = ("board", "crate")

    def local(voltages, gains, channels):
        spectra = front_end(voltages, gains, channels)
        kept = spectra.shape[0]
        split = spectra.reshape(devices, kept // devices, *spectra.shape[1:])
        return correlate(lax.all_to_all(split, axes, 0, 0, tiled=True))

    placed = (P(axes, None), P(None, axes, None), P())
    return jax.shard_map(
        local,
        mesh=mesh,
        in_specs=placed,
        out_specs=P(None, axes, None, None),
        check_vma=False,
    )
```

```python
import math

import jax
import jax.numpy as jnp
import numpy as np
from jax import lax
from jax.experimental import pallas as pl
from jax.experimental.pallas import tpu as pltpu
from jax.sharding import PartitionSpec as P

NFFT = 2048
TAPS = 4
LANES = 128
WIDE = 256
CHUNK = 32
COARSE = 64


def make_window(taps_count, length):
    index = np.arange(taps_count * length, dtype=np.float64)
    centred = (index - taps_count * length / 2 + 0.5) / length
    hamming = 0.54 - 0.46 * np.cos(2.0 * np.pi * index / (taps_count * length - 1))
    return (np.sinc(centred) * hamming).reshape(taps_count, length).astype(np.float32)


def phasor(rows, channels):
    phase = (rows * channels) & (NFFT - 1)
    quarter = NFFT // 4
    turn = (phase + quarter // 2) // quarter
    angle = (phase - turn * quarter).astype(jnp.float32) * (2.0 * math.pi / NFFT)
    square = angle * angle
    sine = angle * (
        1.0 + square * (-1 / 6 + square * (1 / 120 + square * (-1 / 5040 + square * (1 / 362880))))
    )
    cosine = 1.0 + square * (
        -1 / 2
        + square * (1 / 24 + square * (-1 / 720 + square * (1 / 40320 - square * (1 / 3628800))))
    )
    swap = (turn & 1) == 1
    turned_cos = jnp.where(swap, sine, cosine)
    turned_sin = jnp.where(swap, cosine, sine)
    cos_sign = jnp.where(((turn + 1) & 2) == 2, -1.0, 1.0)
    sin_sign = jnp.where((turn & 2) == 2, -1.0, 1.0)
    return turned_cos * cos_sign, turned_sin * sin_sign


def front_kernel(
    v_hbm, window_hbm, channels_hbm, gains_hbm, out,
    volts, window, channels, gains, last_gains, table, first, second, third, raw, turned, sems, small_sems,
):
    inputs = out.shape[2]
    kept = out.shape[0]
    frames = out.shape[3]
    chunks = frames // CHUNK
    span = CHUNK * NFFT
    rows = CHUNK * inputs
    tail = (TAPS - 1) * NFFT
    parts = kept // LANES

    def piece(k):
        at = pl.ds(tail + k * span, span)
        return pltpu.make_async_copy(v_hbm.at[:, at], volts.at[:, at], sems.at[k])

    head = pltpu.make_async_copy(
        v_hbm.at[:, pl.ds(0, tail)], volts.at[:, pl.ds(0, tail)], sems.at[chunks]
    )
    small = [
        pltpu.make_async_copy(source, target, small_sems.at[n])
        for n, (source, target) in enumerate(
            (
                (channels_hbm, channels),
                (window_hbm, window),
                (gains_hbm, gains),
                (gains_hbm, last_gains),
            )
        )
    ]
    small[0].start()
    head.start()
    small[1].start()
    for k in range(chunks):
        piece(k).start()
    small[2].start()
    small[3].start()

    scale = 1.0 / math.sqrt(NFFT)
    steps = NFFT // 2 // COARSE
    small[0].wait()
    for part in range(parts):
        lanes = pl.ds(2 * part * LANES, LANES)
        others = pl.ds((2 * part + 1) * LANES, LANES)
        bins = channels[:, pl.ds(part * LANES, LANES)]
        fine_cos, fine_sin = phasor(lax.broadcasted_iota(jnp.int32, (COARSE, LANES), 0), bins)
        fine_cos, fine_sin = fine_cos * scale, fine_sin * -scale
        coarse_cos, coarse_sin = phasor(
            lax.broadcasted_iota(jnp.int32, (steps, LANES), 0) * COARSE, bins
        )
        sign = jnp.where((bins & 1) == 1, -1.0, 1.0).astype(jnp.bfloat16)
        for a in range(steps):
            cos_a = coarse_cos[a : a + 1]
            sin_a = coarse_sin[a : a + 1]
            real = (fine_cos * cos_a + fine_sin * sin_a).astype(jnp.bfloat16)
            imag = (fine_sin * cos_a - fine_cos * sin_a).astype(jnp.bfloat16)
            table[pl.ds(a * COARSE, COARSE), lanes] = real
            table[pl.ds(a * COARSE, COARSE), others] = imag
            table[pl.ds(NFFT // 2 + a * COARSE, COARSE), lanes] = real * sign
            table[pl.ds(NFFT // 2 + a * COARSE, COARSE), others] = imag * sign

    def filter_tile(k, target, lane):
        taps = [
            jnp.broadcast_to(window[t : t + 1, pl.ds(lane, WIDE)], (inputs, WIDE))
            for t in range(TAPS)
        ]

        def load(f):
            at = (k * CHUNK + f) * NFFT + lane
            if not isinstance(at, int):
                at = pl.multiple_of(at, LANES)
            return volts[:, pl.ds(at, WIDE)].astype(jnp.float32)

        held = [load(f) for f in range(TAPS - 1)]
        for f in range(0, CHUNK, 2):
            pair = []
            for g in (f, f + 1):
                held.append(load(g + TAPS - 1))
                total = taps[0] * held[0]
                for t in range(1, TAPS):
                    total = total + taps[t] * held[t]
                held.pop(0)
                pair.append(total)
            target[pl.ds(f * inputs, 2 * inputs), pl.ds(lane, WIDE)] = jnp.concatenate(
                pair, axis=0
            ).astype(jnp.bfloat16)

    def transform(k, pieces):
        source = slots[k % len(slots)]
        width = 2 * kept // pieces
        at = pl.ds(k * rows, rows)
        for n in range(pieces):
            product = jnp.dot(
                source[...],
                table[:, n * width : (n + 1) * width],
                preferred_element_type=jnp.float32,
            )
            for q in range(width // LANES):
                raw[n * width // LANES + q, at, :] = product[:, q * LANES : (q + 1) * LANES]

    slots = (first, second, third)
    ahead = len(slots) - 1
    small[1].wait()
    head.wait()
    for k in range(ahead):
        piece(k).wait()

        @pl.loop(0, NFFT // WIDE)
        def _(j):
            filter_tile(k, slots[k], pl.multiple_of(j * WIDE, WIDE))

    small[2].wait()
    for k in range(ahead, chunks):
        piece(k).wait()
    for k in range(chunks):
        transform(k, parts if k == chunks - 1 else 1)
        if k + ahead < chunks:
            for j in range(NFFT // WIDE):
                filter_tile(k + ahead, slots[(k + ahead) % len(slots)], j * WIDE)

    def turn(part, block, gains):
        lanes = pl.ds(part * LANES, LANES)
        for i in range(inputs):
            at = pl.ds(block * LANES * inputs + i, LANES, stride=inputs)
            gain_real = gains[0, i : i + 1, lanes]
            gain_imag = gains[1, i : i + 1, lanes]
            real = raw[2 * part, at, :]
            imag = raw[2 * part + 1, at, :]
            turned[0, pl.ds(i, LANES, stride=inputs), :] = (
                gain_real * real - gain_imag * imag
            ).T
            turned[1, pl.ds(i, LANES, stride=inputs), :] = (
                gain_real * imag + gain_imag * real
            ).T
        for side in range(2):
            out[pl.ds(part * LANES, LANES), side, :, pl.ds(block * LANES, LANES)] = (
                turned[side].reshape(LANES, inputs, LANES).astype(jnp.bfloat16)
            )

    turns = [(part, block) for block in range(frames // LANES) for part in range(parts)]
    for part, block in turns[:-1]:
        turn(part, block, gains)
    small[3].wait()
    turn(*turns[-1], last_gains)


def front_end(voltages, gains, channels):
    inputs, samples = voltages.shape
    frames = samples // NFFT - TAPS + 1
    kept = channels.shape[0]
    window = jnp.asarray(make_window(TAPS, NFFT))
    hbm = pl.BlockSpec(memory_space=pltpu.HBM)
    return pl.pallas_call(
        front_kernel,
        out_shape=jax.ShapeDtypeStruct((kept, 2, inputs, frames), jnp.bfloat16),
        in_specs=[hbm] * 4,
        out_specs=pl.BlockSpec(memory_space=pltpu.VMEM),
        scratch_shapes=[
            pltpu.VMEM((inputs, samples), jnp.bfloat16),
            pltpu.VMEM((TAPS, NFFT), jnp.float32),
            pltpu.VMEM((1, kept), jnp.int32),
            *[pltpu.VMEM((2, inputs, kept), jnp.float32)] * 2,
            pltpu.VMEM((NFFT, 2 * kept), jnp.bfloat16),
            *[pltpu.VMEM((CHUNK * inputs, NFFT), jnp.bfloat16)] * 3,
            pltpu.VMEM((2 * kept // LANES, frames * inputs, LANES), jnp.float32),
            pltpu.VMEM((2, LANES * inputs, LANES), jnp.float32),
            pltpu.SemaphoreType.DMA((frames // CHUNK + 1,)),
            pltpu.SemaphoreType.DMA((4,)),
        ],
        compiler_params=pltpu.CompilerParams(vmem_limit_bytes=50 * 2**20),
        cost_estimate=pl.CostEstimate(
            flops=4 * frames * inputs * NFFT * kept,
            bytes_accessed=2 * inputs * samples,
            transcendentals=0,
        ),
        name="front_end",
    )(
        voltages,
        *(
            pltpu.with_memory_space_constraint(x, pltpu.HBM)
            for x in (window, channels.reshape(1, kept), gains)
        ),
    )


def correlate_kernel(spectra, out, rows, blocks, sems):
    sources, owned, _, inputs, frames = spectra.shape
    total = sources * inputs
    side = blocks.shape[-1]
    across = total // side
    contract = (((1,), (1,)), ((), ()))

    def arrange(c):
        real = spectra[:, c, 0].reshape(total, frames)
        imag = spectra[:, c, 1].reshape(total, frames)
        rows[c, 0, :, pl.ds(0, frames)] = real
        rows[c, 0, :, pl.ds(frames, frames)] = imag
        rows[c, 1, :, pl.ds(0, frames)] = imag
        rows[c, 1, :, pl.ds(frames, frames)] = -real

    def copies(c, a, b, slot):
        every = []
        for n, (row, column) in enumerate(((a, b), (b, a)) if a != b else ((a, b),)):
            every.append(
                pltpu.make_async_copy(
                    blocks.at[slot, n],
                    out.at[:, c, pl.ds(row * side, side), pl.ds(column * side, side)],
                    sems.at[slot, n],
                )
            )
        return every

    flying = []
    for c in range(owned):
        arrange(c)
        for b in range(across):
            for a in range(b, across):
                slot = len(flying)
                weights = rows[c, 0, pl.ds(b * side, side), :]
                for part in range(2):
                    block = lax.dot_general(
                        rows[c, part, pl.ds(a * side, side), :],
                        weights,
                        contract,
                        preferred_element_type=jnp.float32,
                    ) / frames
                    blocks[slot, 0, part] = block
                    if a != b:
                        mirror = block.T
                        blocks[slot, 1, part] = mirror if part == 0 else -mirror
                started = copies(c, a, b, slot)
                for copy in started:
                    copy.start()
                flying.append(started)
    for started in flying:
        for copy in started:
            copy.wait()


def correlate(spectra):
    sources, owned, _, inputs, frames = spectra.shape
    total = sources * inputs
    side = 256
    across = total // side
    slots = owned * across * (across + 1) // 2
    return pl.pallas_call(
        correlate_kernel,
        out_shape=jax.ShapeDtypeStruct((2, owned, total, total), jnp.float32),
        in_specs=[pl.BlockSpec(memory_space=pltpu.VMEM)],
        out_specs=pl.BlockSpec(memory_space=pltpu.HBM),
        scratch_shapes=[
            pltpu.VMEM((owned, 2, total, 2 * frames), jnp.bfloat16),
            pltpu.VMEM((slots, 2, 2, side, side), jnp.float32),
            pltpu.SemaphoreType.DMA((slots, 2)),
        ],
        compiler_params=pltpu.CompilerParams(vmem_limit_bytes=48 * 2**20),
        cost_estimate=pl.CostEstimate(
            flops=8 * owned * total * total * frames,
            bytes_accessed=8 * owned * total * total,
            transcendentals=0,
        ),
        name="correlate",
    )(spectra)


def solution(mesh):
    devices = mesh.size
    axes = ("board", "crate")

    def local(voltages, gains, channels):
        spectra = front_end(voltages, gains, channels)
        kept = spectra.shape[0]
        split = spectra.reshape(devices, kept // devices, *spectra.shape[1:])
        return correlate(lax.all_to_all(split, axes, 0, 0, tiled=True))

    placed = (P(axes, None), P(None, axes, None), P())
    return jax.shard_map(
        local,
        mesh=mesh,
        in_specs=placed,
        out_specs=P(None, axes, None, None),
        check_vma=False,
    )
```
